32 devices in a mesh: row: 4 (over x, core), col: 8 (over z, y).
Axes of the slice: x: 2, y: 2, z: 4, core: 2. Of those that a mesh axis runs over, the one named last changes fastest.
Arguments:
- green_vectors: float32 [512, 131072], P('row', 'col'), may hold values from -6 to 6
- amplitudes: float32 [2048, 131072], P('row', 'col'), may hold values from -0.015625 to 0.015625
- cholesky: float32 [2048, 4096], P(('row', 'col')), may hold values from -0.125 to 0.125
Outputs:
- force_bias: float32 [512, 4096], P('col', 'row')
The draws below stay inside these ranges and needn't reach their ends.
All inputs are finite; a program needn't handle non-finite values.
Results may differ from the reference program's by a relative error of at most 0.000084.
Values sent between devices are 32-bit elements; how exact they have to be, the bound alone decides.
A program may use at most 128 MiB of HBM per device.

```python
import jax
import jax.numpy as jnp
from jax import lax

NCHOL = 4096
WALKERS = 512
PAIRS = 131072
SLAB = 2048


def level_of(rng, shape, shards, low, largest):
    def one(position, parts):
        heights = jax.random.uniform(jax.random.fold_in(jax.random.fold_in(rng, 6), position), (parts,), jnp.float32, low / len(shards), largest / len(shards))
        return jnp.repeat(jnp.exp(heights), shape[position] // parts).reshape((-1,) + (1,) * (len(shape) - position - 1))

    factor_of = one(*shards[0])
    for cut in shards[1:]:
        factor_of = factor_of * one(*cut)
    return factor_of


def noise(rng, dims, width, bound, shards=(), dtype=jnp.bfloat16):
    result = width * jax.random.normal(rng, dims, jnp.float32)
    if shards:
        result = result * level_of(rng, dims, shards, -0.22, 0.18)
    return jnp.clip(result, -bound, bound).astype(dtype)


def setup_inputs(seed: int = 0) -> dict:
    arg_keys = jax.random.split(jax.random.key(seed), 4)
    green_vectors = noise(arg_keys[0], (WALKERS, PAIRS), 1.0, 6.0, ((0, 4), (1, 8)), jnp.float32)
    amplitudes = noise(arg_keys[1], (SLAB, PAIRS), PAIRS ** -0.5, 0.015625, ((0, 4), (1, 8)), jnp.float32)
    cholesky = noise(arg_keys[2], (SLAB, NCHOL), SLAB ** -0.5, 0.125, ((0, 32),), jnp.float32)
    return dict(green_vectors=green_vectors, amplitudes=amplitudes, cholesky=cholesky)


def reference(green_vectors, amplitudes, cholesky):
    effective = lax.dot_general(green_vectors, amplitudes, (((1,), (1,)), ((), ())), precision=lax.Precision.HIGHEST, preferred_element_type=jnp.float32)
    return jnp.dot(effective, cholesky, precision=lax.Precision.HIGHEST, preferred_element_type=jnp.float32)
```

```python
import jax
import jax.numpy as jnp
from jax import lax
from jax.sharding import PartitionSpec as P

CHUNKS = 4


def three_pass(left, right, dims):
    return lax.dot_general(
        left,
        right,
        (dims, ((), ())),
        precision=lax.Precision.HIGH,
        preferred_element_type=jnp.float32,
    )


def per_device(green_vectors, amplitudes, cholesky):
    rows = lax.axis_size("row")
    me = lax.axis_index("row")
    held, pairs = green_vectors.shape
    width = pairs // CHUNKS
    sibling = [(i, i ^ 1) for i in range(rows)]

    def part(array, c):
        return lax.slice_in_dim(array, c * width, (c + 1) * width, axis=1)

    far = [
        [
            lax.ppermute(part(green_vectors, c), "row", [(i, (i + hop) % rows) for i in range(rows)])
            for hop in range(2, rows, 2)
        ]
        for c in range(CHUNKS)
    ]
    near = lax.ppermute(green_vectors, "row", sibling)
    stacked = lax.all_gather(cholesky, "col", axis=0, tiled=True)
    last = ((1,), (1,))

    def terms(block, other, slab):
        return three_pass(jnp.concatenate([block, other], axis=0), slab, last)

    sums = [terms(green_vectors, near, amplitudes)]
    for c in range(CHUNKS):
        for at, piece in enumerate(far[c]):
            crossed = lax.ppermute(piece, "row", sibling)
            if c == CHUNKS - 1 and at == 0:
                crossed, stacked = lax.optimization_barrier((crossed, stacked))
            term = terms(piece, crossed, part(amplitudes, c))
            if c == 0:
                sums.append(term)
            else:
                sums[at + 1] += term
    total = jnp.zeros((rows * held, amplitudes.shape[0]), jnp.float32)
    for at, block in enumerate(sums):
        for side in range(2):
            owner = lax.rem(me - 2 * at + rows, rows) ^ side
            total = lax.dynamic_update_slice(
                total, lax.slice_in_dim(block, side * held, (side + 1) * held, axis=0), (owner * held, 0)
            )
    local_walkers = lax.psum_scatter(total, "col", scatter_dimension=0, tiled=True)
    row_terms = three_pass(local_walkers, stacked, ((1,), (0,)))
    return lax.psum_scatter(row_terms, "row", scatter_dimension=1, tiled=True)


def solution(mesh):
    placed = (P("row", "col"), P("row", "col"), P(("row", "col"), None))
    return jax.shard_map(
        per_device, mesh=mesh, in_specs=placed, out_specs=P("col", "row"), check_vma=False
    )
```

```python
import functools

import jax
import jax.numpy as jnp
from jax import lax
from jax.experimental import pallas as pl
from jax.experimental.pallas import tpu as pltpu
from jax.sharding import PartitionSpec as P

SHARES = (6, 5, 3, 2)
MESH = pl.DeviceIdType.MESH


def three_pass(left, right, dims):
    return lax.dot_general(
        left,
        right,
        (dims, ((), ())),
        precision=lax.Precision.HIGH,
        preferred_element_type=jnp.float32,
    )


def halves(x):
    high = x.astype(jnp.bfloat16)
    return high, (x - high.astype(jnp.float32)).astype(jnp.bfloat16)


def tail_kernel(
    rows, cols, total, chol, out, landed, slab, leaving, arrived,
    send_sem, recv_sem, load_sem, row_send, row_recv,
):
    row, col = lax.axis_index("row"), lax.axis_index("col")
    quarter = out.shape[1]
    walkers = out.shape[0]

    barrier = pltpu.get_barrier_semaphore()
    for k in range(1, cols):
        pl.semaphore_signal(barrier, inc=1, device_id=(row, lax.rem(col + k, cols)), device_id_type=MESH)
    for m in range(1, rows):
        pl.semaphore_signal(barrier, inc=1, device_id=(lax.rem(row + m, rows), col), device_id_type=MESH)
    order = [rows // 2] + [m for m in range(1, rows) if m != rows // 2] + [0]
    loads = {}
    for m in order:
        start = pl.multiple_of(lax.rem(row + m, rows) * quarter, quarter)
        loads[m] = pltpu.make_async_copy(chol.at[:, pl.ds(start, quarter)], slab.at[m], load_sem.at[m])
    own = pltpu.make_async_copy(total.at[col], landed.at[0], recv_sem.at[0])
    own.start()
    for m in order:
        loads[m].start()
    pl.semaphore_wait(barrier, rows + cols - 2)

    copies = []
    for k in range(1, cols):
        target = lax.rem(col + k, cols)
        copy = pltpu.make_async_remote_copy(
            src_ref=total.at[target],
            dst_ref=landed.at[k],
            send_sem=send_sem.at[k],
            recv_sem=recv_sem.at[k],
            device_id=(row, target),
            device_id_type=MESH,
        )
        copy.start()
        copies.append(copy)
    own.wait()
    effective = landed[0]
    for k, copy in enumerate(copies):
        copy.wait_recv()
        effective = effective + landed[k + 1]
    high, low = halves(effective)
    both = jnp.concatenate([high, low], axis=0)

    tile = min(512, quarter)
    sends = []
    for m in order:
        loads[m].wait()
        for t in range(0, quarter, tile):
            right_high, right_low = halves(slab[m, :, t : t + tile])
            pair = jnp.dot(both, right_high, preferred_element_type=jnp.float32)
            rest = jnp.dot(high, right_low, preferred_element_type=jnp.float32)
            leaving[m, :, t : t + tile] = pair[:walkers] + (pair[walkers:] + rest)
        if m:
            send = pltpu.make_async_remote_copy(
                src_ref=leaving.at[m],
                dst_ref=arrived.at[m],
                send_sem=row_send.at[m],
                recv_sem=row_recv.at[m],
                device_id=(lax.rem(row + m, rows), col),
                device_id_type=MESH,
            )
            send.start()
            sends.append((m, send))
    result = leaving[0]
    for m, send in sends:
        send.wait_recv()
        result = result + arrived[m]
    out[...] = result
    for copy in copies:
        copy.wait_send()
    for m, send in sends:
        send.wait_send()


def tail(total, chol):
    rows, cols = lax.axis_size("row"), lax.axis_size("col")
    walkers, depth = total.shape[0] // cols, total.shape[1]
    quarter = chol.shape[1] // rows
    f32 = jnp.float32
    return pl.pallas_call(
        functools.partial(tail_kernel, rows, cols),
        out_shape=jax.ShapeDtypeStruct((walkers, quarter), f32),
        in_specs=[pl.BlockSpec(memory_space=pl.ANY)] * 2,
        out_specs=pl.BlockSpec(memory_space=pltpu.VMEM),
        scratch_shapes=[
            pltpu.VMEM((cols, walkers, depth), f32),
            pltpu.VMEM((rows, depth, quarter), f32),
            pltpu.VMEM((rows, walkers, quarter), f32),
            pltpu.VMEM((rows, walkers, quarter), f32),
            pltpu.SemaphoreType.DMA((cols,)),
            pltpu.SemaphoreType.DMA((cols,)),
            pltpu.SemaphoreType.DMA((rows,)),
            pltpu.SemaphoreType.DMA((rows,)),
            pltpu.SemaphoreType.DMA((rows,)),
        ],
        compiler_params=pltpu.CompilerParams(
            collective_id=0, has_side_effects=True, vmem_limit_bytes=32 * 1024 * 1024
        ),
    )(total.reshape(cols, walkers, depth), chol)


def per_device(green_vectors, amplitudes, cholesky):
    rows = lax.axis_size("row")
    me = lax.axis_index("row")
    held, pairs = green_vectors.shape
    sibling = [(i, i ^ 1) for i in range(rows)]
    hops = range(2, rows, 2)
    cuts = [0]
    for share in SHARES:
        cuts.append(cuts[-1] + share * pairs // sum(SHARES))

    def part(array, c):
        return lax.slice_in_dim(array, cuts[c], cuts[c + 1], axis=1)

    def far(piece):
        return [lax.ppermute(piece, "row", [(i, (i + hop) % rows) for i in range(rows)]) for hop in hops]

    def terms(block, other, slab):
        return three_pass(jnp.concatenate([block, other], axis=0), slab, ((1,), (1,)))

    def cross(pieces):
        return [lax.ppermute(piece, "row", sibling) for piece in pieces]

    def dots(pieces, crossed, c):
        return [terms(a, b, part(amplitudes, c)) for a, b in zip(pieces, crossed)]

    first, second = far(part(green_vectors, 0)), far(part(green_vectors, 1))
    stacked = lax.all_gather(cholesky, "col", axis=0, tiled=True)
    near = lax.ppermute(green_vectors, "row", sibling)
    own = terms(green_vectors, near, amplitudes)
    piece, own = lax.optimization_barrier((part(green_vectors, 2), own))
    third = far(piece)
    second, own = lax.optimization_barrier((second, own))
    sums = dots(first, cross(first), 0)
    piece, sums = lax.optimization_barrier((part(green_vectors, 3), sums))
    fourth = far(piece)
    third, sums = lax.optimization_barrier((third, sums))
    for c, pieces in ((1, second), (2, third)):
        sums = [a + b for a, b in zip(sums, dots(pieces, cross(pieces), c))]
        if c == 2:
            fourth, sums, stacked = lax.optimization_barrier((fourth, sums, stacked))
    sums = [a + b for a, b in zip(sums, dots(fourth, cross(fourth), 3))]

    total = jnp.zeros((rows * held, amplitudes.shape[0]), jnp.float32)
    for at, block in enumerate([own] + sums):
        for side in range(2):
            owner = lax.rem(me - 2 * at + rows, rows) ^ side
            total = lax.dynamic_update_slice(
                total, lax.slice_in_dim(block, side * held, (side + 1) * held, axis=0), (owner * held, 0)
            )
    return tail(total, stacked)


def solution(mesh):
    placed = (P("row", "col"), P("row", "col"), P(("row", "col"), None))
    return jax.shard_map(
        per_device, mesh=mesh, in_specs=placed, out_specs=P("col", "row"), check_vma=False
    )
```

```python
import functools

import jax
import jax.numpy as jnp
from jax import lax
from jax.experimental import pallas as pl
from jax.experimental.pallas import tpu as pltpu
from jax.sharding import PartitionSpec as P

SHARES = (6, 5, 3, 2)
MESH = pl.DeviceIdType.MESH


def three_pass(left, right, dims):
    return lax.dot_general(
        left,
        right,
        (dims, ((), ())),
        precision=lax.Precision.HIGH,
        preferred_element_type=jnp.float32,
    )


def halves(x):
    high = x.astype(jnp.bfloat16)
    return high, (x - high.astype(jnp.float32)).astype(jnp.bfloat16)


def tail_kernel(
    rows, cols, total, chol, out, landed, slab, leaving, arrived,
    send_sem, recv_sem, load_sem, row_send, row_recv,
):
    row, col = lax.axis_index("row"), lax.axis_index("col")
    quarter = out.shape[1]
    walkers = out.shape[0]

    barrier = pltpu.get_barrier_semaphore()
    for k in range(1, cols):
        pl.semaphore_signal(barrier, inc=1, device_id=(row, lax.rem(col + k, cols)), device_id_type=MESH)
    for m in range(1, rows):
        pl.semaphore_signal(barrier, inc=1, device_id=(lax.rem(row + m, rows), col), device_id_type=MESH)
    order = [rows // 2] + [m for m in range(1, rows) if m != rows // 2] + [0]
    loads = {}
    for m in order:
        start = pl.multiple_of(lax.rem(row + m, rows) * quarter, quarter)
        loads[m] = pltpu.make_async_copy(chol.at[:, pl.ds(start, quarter)], slab.at[m], load_sem.at[m])
    own = pltpu.make_async_copy(total.at[col], landed.at[0], recv_sem.at[0])
    own.start()
    for m in order:
        loads[m].start()
    pl.semaphore_wait(barrier, rows + cols - 2)

    copies = []
    for k in range(1, cols):
        target = lax.rem(col + k, cols)
        copy = pltpu.make_async_remote_copy(
            src_ref=total.at[target],
            dst_ref=landed.at[k],
            send_sem=send_sem.at[k],
            recv_sem=recv_sem.at[k],
            device_id=(row, target),
            device_id_type=MESH,
        )
        copy.start()
        copies.append(copy)
    own.wait()
    effective = landed[0]
    for k, copy in enumerate(copies):
        copy.wait_recv()
        effective = effective + landed[k + 1]
    high, low = halves(effective)
    both = jnp.concatenate([high, low], axis=0)

    tile = min(512, quarter)
    sends = []
    for m in order:
        loads[m].wait()
        for t in range(0, quarter, tile):
            right_high, right_low = halves(slab[m, :, t : t + tile])
            pair = jnp.dot(both, right_high, preferred_element_type=jnp.float32)
            rest = jnp.dot(high, right_low, preferred_element_type=jnp.float32)
            leaving[m, :, t : t + tile] = pair[:walkers] + (pair[walkers:] + rest)
        if m:
            send = pltpu.make_async_remote_copy(
                src_ref=leaving.at[m],
                dst_ref=arrived.at[m],
                send_sem=row_send.at[m],
                recv_sem=row_recv.at[m],
                device_id=(lax.rem(row + m, rows), col),
                device_id_type=MESH,
            )
            send.start()
            sends.append((m, send))
    result = leaving[0]
    for m, send in sends:
        send.wait_recv()
        result = result + arrived[m]
    out[...] = result
    for copy in copies:
        copy.wait_send()
    for m, send in sends:
        send.wait_send()


def tail(total, chol):
    rows, cols = lax.axis_size("row"), lax.axis_size("col")
    walkers, depth = total.shape[0] // cols, total.shape[1]
    quarter = chol.shape[1] // rows
    f32 = jnp.float32
    return pl.pallas_call(
        functools.partial(tail_kernel, rows, cols),
        out_shape=jax.ShapeDtypeStruct((walkers, quarter), f32),
        in_specs=[pl.BlockSpec(memory_space=pl.ANY)] * 2,
        out_specs=pl.BlockSpec(memory_space=pltpu.VMEM),
        scratch_shapes=[
            pltpu.VMEM((cols, walkers, depth), f32),
            pltpu.VMEM((rows, depth, quarter), f32),
            pltpu.VMEM((rows, walkers, quarter), f32),
            pltpu.VMEM((rows, walkers, quarter), f32),
            pltpu.SemaphoreType.DMA((cols,)),
            pltpu.SemaphoreType.DMA((cols,)),
            pltpu.SemaphoreType.DMA((rows,)),
            pltpu.SemaphoreType.DMA((rows,)),
            pltpu.SemaphoreType.DMA((rows,)),
        ],
        compiler_params=pltpu.CompilerParams(
            collective_id=0, has_side_effects=True, vmem_limit_bytes=32 * 1024 * 1024
        ),
    )(total.reshape(cols, walkers, depth), chol)


def per_device(green_vectors, amplitudes, cholesky):
    rows = lax.axis_size("row")
    me = lax.axis_index("row")
    held, pairs = green_vectors.shape
    sibling = [(i, i ^ 1) for i in range(rows)]
    hops = range(2, rows, 2)
    cuts = [0]
    for share in SHARES:
        cuts.append(cuts[-1] + share * pairs // sum(SHARES))

    def part(array, c):
        return lax.slice_in_dim(array, cuts[c], cuts[c + 1], axis=1)

    def far(piece):
        return [lax.ppermute(piece, "row", [(i, (i + hop) % rows) for i in range(rows)]) for hop in hops]

    def terms(block, other, slab):
        return three_pass(jnp.concatenate([block, other], axis=0), slab, ((1,), (1,)))

    def cross(pieces):
        return [lax.ppermute(piece, "row", sibling) for piece in pieces]

    def dots(pieces, crossed, c):
        return [terms(a, b, part(amplitudes, c)) for a, b in zip(pieces, crossed)]

    first, second = far(part(green_vectors, 0)), far(part(green_vectors, 1))
    cols = lax.axis_size("col")
    place = lax.axis_index("col")
    pairing = [(i, i ^ 1) for i in range(cols)]
    along = [
        lax.ppermute(cholesky, "col", [(i, (i + hop) % cols) for i in range(cols)])
        for hop in range(2, cols, 2)
    ]
    beside = [lax.ppermute(cholesky, "col", pairing)]
    near = lax.ppermute(green_vectors, "row", sibling)
    own = terms(green_vectors, near, amplitudes)
    third = far(part(green_vectors, 2))
    second, along, own = lax.optimization_barrier((second, along, own))
    beside += [lax.ppermute(piece, "col", pairing) for piece in along]
    deep = cholesky.shape[0]
    stacked = jnp.zeros((cols * deep, cholesky.shape[1]), jnp.float32)
    for at, both in enumerate(zip([cholesky] + along, beside)):
        for side, piece in enumerate(both):
            owner = lax.rem((place ^ side) - 2 * at + cols, cols)
            stacked = lax.dynamic_update_slice(stacked, piece, (owner * deep, 0))
    sums = dots(first, cross(first), 0)
    piece, sums = lax.optimization_barrier((part(green_vectors, 3), sums))
    fourth = far(piece)
    third, sums = lax.optimization_barrier((third, sums))
    for c, pieces in ((1, second), (2, third)):
        sums = [a + b for a, b in zip(sums, dots(pieces, cross(pieces), c))]
        if c == 2:
            fourth, sums, stacked = lax.optimization_barrier((fourth, sums, stacked))
    sums = [a + b for a, b in zip(sums, dots(fourth, cross(fourth), 3))]

    total = jnp.zeros((rows * held, amplitudes.shape[0]), jnp.float32)
    for at, block in enumerate([own] + sums):
        for side in range(2):
            owner = lax.rem(me - 2 * at + rows, rows) ^ side
            total = lax.dynamic_update_slice(
                total, lax.slice_in_dim(block, side * held, (side + 1) * held, axis=0), (owner * held, 0)
            )
    return tail(total, stacked)


def solution(mesh):
    placed = (P("row", "col"), P("row", "col"), P(("row", "col"), None))
    return jax.shard_map(
        per_device, mesh=mesh, in_specs=placed, out_specs=P("col", "row"), check_vma=False
    )
```
